512 devices in a mesh: rep: 16 (over z_hi, x, core), hid: 32 (over z_lo, y).
Axes of the slice: x: 4, y: 4, z: 16 (z_hi: 2, z_lo: 8; z = z_hi * 8 + z_lo), core: 2. Of those that a mesh axis runs over, the one named last changes fastest.
Arguments:
- tokens: bfloat16 [4096, 8192], P('rep', 'hid'), may hold values from -6 to 6
- cotangent: bfloat16 [4096, 8192], P('rep', 'hid'), may hold values from -6 to 6
- seq_ids: int32 [16, 256], P('rep'), may hold values from 0 to 7, never falling along the last dimension, each value on 1 to 64 neighbouring positions
- in_blocks: int32 [128, 5], P('hid'), may hold values from 0 to 63, as said below
- out_blocks: int32 [128, 5], P('hid'), may hold values from 0 to 63, as said below
- unit_scale: float32 [16384], P('hid'), may hold values from 0.3 to 3.2
- gate_weight: bfloat16 [128, 5, 128, 128], P('hid'), may hold values from -6 to 6
- up_weight: bfloat16 [128, 5, 128, 128], P('hid'), may hold values from -6 to 6
- down_weight: bfloat16 [128, 5, 128, 128], P('hid'), may hold values from -6 to 6
Outputs:
- new_gate: bfloat16 [128, 5, 128, 128], P('hid')
- new_up: bfloat16 [128, 5, 128, 128], P('hid')
- new_down: bfloat16 [128, 5, 128, 128], P('hid')
The draws below stay inside these ranges and needn't reach their ends.
Inputs may be any that keep to these rules, and one draw needn't show every extreme that they name: `in_blocks`: each row lists 5 different blocks, and every block appears in some row. `out_blocks`: each row lists 5 different blocks, and every block appears in some row. `seq_ids`: ids never fall along a row; each sequence has 1 to 64 tokens.
All inputs are finite; a program needn't handle non-finite values.
Results may differ from the reference program's by a relative error of at most 0.0075.
Values may be sent and summed in bfloat16 or wider, within the bound.
No kernel may reach another device: no remote copies, remote signals or barrier semaphores. Data moves between devices by JAX's collectives and lax.ppermute only.
A program may use at most 64 MiB of HBM per device.

```python
import math
import jax
import jax.numpy as jnp
import numpy as np
from jax import lax

D = 8192
FF = 16384
BLOCK = 128
LEVELS = 5
SEGS = 8
TOK_REP = 256
MOST_LEN = 64
NB_D = 64
NB_H = 128
TOKENS = 4096
N_REP = 16


def butterfly_rows(key):
    first, second = jax.random.split(key)
    block_perm = jax.random.permutation(first, NB_D)
    base = jax.random.permutation(second, NB_H) % NB_D
    strides = jnp.array([0, 1, 4, NB_D // 4, NB_D // 2], dtype=jnp.int32)
    position = jnp.bitwise_xor(base[:, None].astype(jnp.int32), strides[None, :])
    return block_perm[position].astype(jnp.int32)


def draw_in_blocks(key, part):
    return butterfly_rows(jax.random.fold_in(key, 101))


def draw_out_blocks(key, part):
    return butterfly_rows(jax.random.fold_in(key, 202))


def draw_unit_scale(key, part):
    inner = jax.random.fold_in(key, 303)
    ramp = jnp.arange(FF, dtype=jnp.float32) / FF
    rough = jax.random.uniform(inner, (FF,), jnp.float32, 0.75, 1.35)
    values = (0.6 + 1.2 * ramp) * rough
    return values.astype(jnp.float32)


def block_scale(own_key, dims, cuts, smallest, high):
    def one(dim, parts):
        steps = jax.random.uniform(jax.random.fold_in(jax.random.fold_in(own_key, 6), dim), (parts,), jnp.float32, smallest / len(cuts), high / len(cuts))
        return jnp.repeat(jnp.exp(steps), dims[dim] // parts).reshape((-1,) + (1,) * (len(dims) - dim - 1))

    factor_of = one(*cuts[0])
    for cut in cuts[1:]:
        factor_of = factor_of * one(*cut)
    return factor_of


def profile(number_of, total, bound, lean):
    loads = [(1 << 20) // math.isqrt(grade ** lean) + 1 for grade in range(2, number_of + 1)]
    spare, given = total - bound - (number_of - 1), [1] * (number_of - 1)
    while spare > 0:
        free = [i for i in range(number_of - 1) if given[i] < bound]
        mass, remaining = sum([loads[i] for i in free]), spare
        for i in free:
            more = min(bound - given[i], max(1, remaining * loads[i] // mass), spare)
            given[i] = given[i] + more
            spare = spare - more
    return np.array([bound] + given)


def ragged(stream_key, number_of, total, most, slope):
    if number_of == 2:
        one = jax.random.randint(stream_key, (), max(1, total - most), min(most, total - 1) + 1)
        return jnp.stack([one, total - one])
    lengths = jnp.asarray(profile(number_of, total, most, slope), jnp.int32)
    twos = (number_of - 1) // 2
    giver, receiver = lengths[1:1 + 2 * twos:2], lengths[2:2 + 2 * twos:2]
    slack = jnp.minimum(giver - 1, most - receiver)
    moved = jax.random.randint(jax.random.fold_in(stream_key, 1), (twos,), 0, 1 << 20) % (slack + 1)
    lengths = lengths.at[1:1 + 2 * twos:2].set(giver - moved).at[2:2 + 2 * twos:2].set(receiver + moved)
    return lengths[jax.random.permutation(jax.random.fold_in(stream_key, 2), number_of)]


def centred(rng, dims, deviation, reach, pieces=(), held_as=jnp.bfloat16):
    entries = deviation * jax.random.normal(rng, dims, jnp.float32)
    if pieces:
        entries = entries * block_scale(rng, dims, pieces, -0.22, 0.18)
    return jnp.clip(entries, -reach, reach).astype(held_as)


def setup_inputs(seed: int = 0) -> dict:
    streams_of = jax.random.split(jax.random.key(seed), 10)
    return {
        "tokens": centred(streams_of[0], (TOKENS, D), 1.0, 6.0, ((0, 16), (1, 32))),
        "cotangent": centred(streams_of[1], (TOKENS, D), 1.0, 6.0, ((0, 16), (1, 32))),
        "seq_ids": jax.vmap(lambda own: jnp.searchsorted(jnp.cumsum(ragged(own, SEGS, TOK_REP, MOST_LEN, 0)), jnp.arange(TOK_REP), side="right"))(jax.random.split(streams_of[2], N_REP)).reshape((N_REP, TOK_REP)).astype(jnp.int32),
        "in_blocks": draw_in_blocks(jax.random.fold_in(streams_of[9], 71), 0),
        "out_blocks": draw_out_blocks(jax.random.fold_in(streams_of[9], 71), 0),
        "unit_scale": draw_unit_scale(jax.random.fold_in(streams_of[9], 71), 0),
        "gate_weight": centred(streams_of[6], (NB_H, LEVELS, BLOCK, BLOCK), 1.0, 6.0, ((0, 32),)),
        "up_weight": centred(streams_of[7], (NB_H, LEVELS, BLOCK, BLOCK), 1.0, 6.0, ((0, 32),)),
        "down_weight": centred(streams_of[8], (NB_H, LEVELS, BLOCK, BLOCK), 1.0, 6.0, ((0, 32),)),
    }


learn_rate = 8.0
max_rms = 0.1

def replica_grads(tok_rows, cot_rows, seq_row, in_blocks, out_blocks, unit_scale, gate_weight, up_weight, down_weight):
    same_seq = (seq_row[:, None] == seq_row[None, :]).astype(jnp.float32)
    seq_len = lax.optimization_barrier(jnp.sum(same_seq, axis=1))
    tok_weight = TOK_REP / (SEGS * seq_len)
    scaled = (cot_rows.astype(jnp.float32) * tok_weight[:, None]).astype(jnp.bfloat16)
    hidden_blocks = FF // BLOCK
    in_scale = (LEVELS * BLOCK) ** (-0.5)
    out_scale = (LEVELS * BLOCK * (FF // D)) ** (-0.5)
    picked = jnp.take(tok_rows.reshape(TOK_REP, D // BLOCK, BLOCK), in_blocks.reshape(-1), axis=1)
    picked = picked.reshape(TOK_REP, hidden_blocks, LEVELS, BLOCK).astype(jnp.float32)
    gate_pre = jnp.einsum('thlc,hlcd->thd', picked, gate_weight.astype(jnp.float32)) * in_scale
    up_pre = jnp.einsum('thlc,hlcd->thd', picked, up_weight.astype(jnp.float32)) * in_scale
    unit_gain = unit_scale.reshape(hidden_blocks, BLOCK)
    sigmoid_gate = jax.nn.sigmoid(gate_pre)
    silu_gate = gate_pre * sigmoid_gate
    hidden = (silu_gate * up_pre * unit_gain).astype(jnp.bfloat16)
    picked_cot = jnp.take(scaled.reshape(TOK_REP, D // BLOCK, BLOCK), out_blocks.reshape(-1), axis=1)
    picked_cot = picked_cot.reshape(TOK_REP, hidden_blocks, LEVELS, BLOCK).astype(jnp.float32)
    d_hidden = jnp.einsum('thlo,hlio->thi', picked_cot, down_weight.astype(jnp.float32)) * out_scale
    grad_down = jnp.einsum('thi,thlo->hlio', hidden.astype(jnp.float32), picked_cot) * out_scale
    d_scaled = d_hidden * unit_gain
    d_gate = (d_scaled * up_pre * sigmoid_gate * (1.0 + gate_pre * (1.0 - sigmoid_gate))).astype(jnp.bfloat16)
    d_up = (d_scaled * silu_gate).astype(jnp.bfloat16)
    grad_gate = jnp.einsum('thlc,thd->hlcd', picked, d_gate.astype(jnp.float32)) * in_scale
    grad_up = jnp.einsum('thlc,thd->hlcd', picked, d_up.astype(jnp.float32)) * in_scale
    sq_total = jnp.sum(grad_gate * grad_gate) + jnp.sum(grad_up * grad_up) + jnp.sum(grad_down * grad_down)
    count_all = 3 * hidden_blocks * LEVELS * BLOCK * BLOCK
    rms_value = jnp.sqrt(sq_total / count_all + 1e-06)
    clip = jnp.minimum(1.0, max_rms / rms_value)
    step_size = -learn_rate * clip
    return (grad_gate * step_size, grad_up * step_size, grad_down * step_size)

def reference(tokens, cotangent, seq_ids, in_blocks, out_blocks, unit_scale, gate_weight, up_weight, down_weight):
    tok_split = tokens.reshape(N_REP, TOK_REP, D)
    cot_split = cotangent.reshape(N_REP, TOK_REP, D)

    def accumulate(carry, items):
        tok_rows, cot_rows, seq_row = items
        deltas = replica_grads(tok_rows, cot_rows, seq_row, in_blocks, out_blocks, unit_scale, gate_weight, up_weight, down_weight)
        return ((carry[0] + deltas[0], carry[1] + deltas[1], carry[2] + deltas[2]), None)
    shape = gate_weight.shape
    start = (jnp.zeros(shape, jnp.float32), jnp.zeros(shape, jnp.float32), jnp.zeros(shape, jnp.float32))
    totals, _ = lax.scan(accumulate, start, (tok_split, cot_split, seq_ids))
    new_gate = (gate_weight.astype(jnp.float32) + totals[0] / N_REP).astype(jnp.bfloat16)
    new_up = (up_weight.astype(jnp.float32) + totals[1] / N_REP).astype(jnp.bfloat16)
    new_down = (down_weight.astype(jnp.float32) + totals[2] / N_REP).astype(jnp.bfloat16)
    return (new_gate, new_up, new_down)
```

```python
import jax
import jax.numpy as jnp
from jax import lax
from jax.experimental import pallas as pl
from jax.experimental.pallas import tpu as pltpu
from jax.sharding import PartitionSpec as P

D = 8192
FF = 16384
BLOCK = 128
LEVELS = 5
SEGS = 8
NZ, NY = 8, 4
NH, NX, NC = 2, 4, 2
learn_rate = 8.0
max_rms = 0.1


def hid_pairs(move):
    pairs = []
    for z in range(NZ):
        for y in range(NY):
            to = move(z, y)
            if to is not None:
                pairs.append((z * NY + y, to[0] * NY + to[1]))
    return pairs


def rep_id(h, x, c):
    return (h * NX + x) * NC + c


def rep_pairs(move):
    return [
        (rep_id(h, x, c), rep_id(*move(h, x, c)))
        for h in range(NH)
        for x in range(NX)
        for c in range(NC)
    ]


def up_pairs(step):
    return hid_pairs(lambda z, y: (z + 1, y) if step - 1 <= z < NZ - 1 else None)


def down_pairs(step):
    return hid_pairs(lambda z, y: (z - 1, y) if 0 < z <= NZ - step else None)


Y_NEXT = hid_pairs(lambda z, y: (z, (y + 1) % NY))
Y_PREV = hid_pairs(lambda z, y: (z, (y - 1) % NY))
CORE = rep_pairs(lambda h, x, c: (h, x, 1 - c))
ZHI = rep_pairs(lambda h, x, c: (1 - h, x, c))
Y_GROUPS = [[z * NY + y for y in range(NY)] for z in range(NZ)]
Z_GROUPS = [[z * NY + y for z in range(NZ)] for y in range(NY)]
X_GROUPS = [[rep_id(h, x, c) for x in range(NX)] for h in range(NH) for c in range(NC)]


def y_ring(own):
    half = own.shape[0] // 2
    left = lax.ppermute(own, "hid", Y_NEXT)
    right = lax.ppermute(own, "hid", Y_PREV)
    far_a = lax.ppermute(left[:half], "hid", Y_NEXT)
    far_b = lax.ppermute(right[half:], "hid", Y_PREV)
    return own, right, far_a, far_b, left


def ffn_kernel(in_scale, out_scale, n_bufs, at_in, at_out, *refs):
    bufs = refs[:n_bufs]
    wg, wu, wd, gain, grads, sq_out, big, sems = refs[n_bufs:]
    start, copies = 0, []
    for k, buf in enumerate(bufs):
        n = buf.shape[0]
        copies.append(pltpu.make_async_copy(buf, big.at[pl.ds(start, n)], sems.at[k]))
        start += n
    for copy in copies:
        copy.start()
    for copy in copies:
        copy.wait()
    acc = jnp.zeros((1, 1), jnp.float32)
    for h in range(wg.shape[0]):
        x = jnp.concatenate([big[at_in[h, l]] for l in range(LEVELS)], axis=1)
        s = jnp.concatenate([big[at_out[h, l]] for l in range(LEVELS)], axis=1)
        w_in = jnp.concatenate(
            [wg[h].reshape(LEVELS * BLOCK, BLOCK), wu[h].reshape(LEVELS * BLOCK, BLOCK)], axis=1
        )
        pre = jnp.dot(x, w_in, preferred_element_type=jnp.float32) * in_scale
        gate, up = pre[:, :BLOCK], pre[:, BLOCK:]
        g = gain[h]
        sig = jax.nn.sigmoid(gate)
        silu = gate * sig
        hidden = (silu * up * g).astype(jnp.bfloat16)
        w_out = jnp.concatenate([wd[h, l] for l in range(LEVELS)], axis=1)
        d_hidden = (
            lax.dot_general(s, w_out, (((1,), (1,)), ((), ())), preferred_element_type=jnp.float32)
            * out_scale
        )
        g_down = (
            lax.dot_general(hidden, s, (((0,), (0,)), ((), ())), preferred_element_type=jnp.float32)
            * out_scale
        )
        d_scaled = d_hidden * g
        d_gate = (d_scaled * up * sig * (1.0 + gate * (1.0 - sig))).astype(jnp.bfloat16)
        d_up = (d_scaled * silu).astype(jnp.bfloat16)
        d_both = jnp.concatenate([d_gate, d_up], axis=1)
        g_in = (
            lax.dot_general(x, d_both, (((0,), (0,)), ((), ())), preferred_element_type=jnp.float32)
            * in_scale
        )
        acc = acc + jnp.sum(jnp.sum(g_in * g_in, axis=0, keepdims=True), axis=1, keepdims=True)
        acc = acc + jnp.sum(jnp.sum(g_down * g_down, axis=0, keepdims=True), axis=1, keepdims=True)
        for l in range(LEVELS):
            rows = slice(l * BLOCK, (l + 1) * BLOCK)
            grads[0, h, l] = g_in[rows, :BLOCK].astype(jnp.bfloat16)
            grads[1, h, l] = g_in[rows, BLOCK:].astype(jnp.bfloat16)
            grads[2, h, l] = g_down[:, rows].astype(jnp.bfloat16)
    sq_out[...] = jnp.broadcast_to(acc, sq_out.shape)


def per_device(
    tokens,
    cotangent,
    seq_ids,
    in_blocks,
    out_blocks,
    unit_scale,
    gate_weight,
    up_weight,
    down_weight,
):
    tok_count = tokens.shape[0]
    blocks_dev = gate_weight.shape[0]
    hid, rep = lax.axis_index("hid"), lax.axis_index("rep")
    z, y = hid // NY, hid % NY
    core, x = rep % NC, (rep // NC) % NX

    same_seq = (seq_ids[0][:, None] == seq_ids[0][None, :]).astype(jnp.float32)
    seq_len = jnp.sum(same_seq, axis=1)
    tok_weight = tok_count / (SEGS * seq_len)
    scaled = (cotangent.astype(jnp.float32) * tok_weight[:, None]).astype(jnp.bfloat16)

    def by_block(a):
        return a.reshape(tok_count, -1, BLOCK).transpose(1, 0, 2)

    own = jnp.concatenate([by_block(tokens), by_block(scaled)], axis=0)
    per_plane = own.shape[0]
    local = per_plane // 2
    ups, downs = [own], [own]
    for step in range(1, NZ):
        ups.append(lax.ppermute(ups[-1], "hid", up_pairs(step)))
        downs.append(lax.ppermute(downs[-1], "hid", down_pairs(step)))
    first = jnp.clip(z - 2, 0, NZ // 2)
    near = jnp.concatenate(ups[3:0:-1] + downs[:4], axis=0)
    window = lax.dynamic_slice_in_dim(near, (3 - z + first) * per_plane, 4 * per_plane, 0)
    later = [
        jnp.where(z + k < NZ, downs[k], ups[NZ - k]) if 0 < k < NZ else None for k in range(1, NZ)
    ]
    rest = lax.dynamic_slice_in_dim(
        jnp.concatenate(later, axis=0), (first + 3 - z) * per_plane, 4 * per_plane, 0
    )
    bufs = y_ring(window) + y_ring(rest)

    def place(blocks, kind):
        owner = blocks // local
        slot = (owner // NY - first) % NZ
        side = (owner % NY - y) % NY
        return (((slot // 4) * NY + side) * 4 + slot % 4) * per_plane + kind * local + blocks % local

    any_spec = pl.BlockSpec(memory_space=pl.ANY)
    vmem = pl.BlockSpec(memory_space=pltpu.VMEM)
    smem = pl.BlockSpec(memory_space=pltpu.SMEM)
    in_scale = (LEVELS * BLOCK) ** (-0.5)
    out_scale = (LEVELS * BLOCK * (FF // D)) ** (-0.5)

    def kernel(*refs):
        ffn_kernel(in_scale, out_scale, len(bufs), *refs)

    grads, local_sq = pl.pallas_call(
        kernel,
        out_shape=(
            jax.ShapeDtypeStruct((3, *gate_weight.shape), jnp.bfloat16),
            jax.ShapeDtypeStruct((8, BLOCK), jnp.float32),
        ),
        in_specs=[smem, smem] + [any_spec] * len(bufs) + [vmem] * 4,
        out_specs=(vmem, vmem),
        scratch_shapes=[
            pltpu.VMEM((sum(b.shape[0] for b in bufs), tok_count, BLOCK), jnp.bfloat16),
            pltpu.SemaphoreType.DMA((len(bufs),)),
        ],
        compiler_params=pltpu.CompilerParams(vmem_limit_bytes=40 << 20),
        name="ffn",
    )(
        place(in_blocks, 0),
        place(out_blocks, 1),
        *bufs,
        gate_weight,
        up_weight,
        down_weight,
        unit_scale.reshape(blocks_dev, 1, BLOCK),
    )

    replicas = NH * NX * NC
    rows = 3 * blocks_dev * LEVELS * BLOCK
    share = rows // (NC * NX)
    halves = grads.reshape(NC, rows // NC, BLOCK)
    mine = lax.dynamic_index_in_dim(halves, core, 0, keepdims=False)
    partner = lax.ppermute(
        lax.dynamic_index_in_dim(halves, 1 - core, 0, keepdims=False), "rep", CORE
    )
    sums = jnp.stack([local_sq, lax.ppermute(local_sq, "rep", CORE)])
    for groups in (Y_GROUPS, Z_GROUPS):
        n = len(groups[0])
        every = lax.all_to_all(
            jnp.broadcast_to(sums[None], (n, *sums.shape)),
            "hid",
            0,
            0,
            axis_index_groups=groups,
            tiled=True,
        )
        sums = every.sum(axis=0)
    count_all = 3 * (FF // BLOCK) * LEVELS * BLOCK * BLOCK
    rms_value = jnp.sqrt(sums[:, 0, 0] / count_all + 1e-06)
    step_size = -learn_rate * jnp.minimum(1.0, max_rms / rms_value)
    pair = (
        mine.astype(jnp.float32) * step_size[0] + partner.astype(jnp.float32) * step_size[1]
    ).astype(jnp.bfloat16)
    pieces = lax.all_to_all(
        pair.reshape(NX, share, BLOCK), "rep", 0, 0, axis_index_groups=X_GROUPS, tiled=True
    )
    part = pieces.astype(jnp.float32).sum(axis=0).astype(jnp.bfloat16)
    other = lax.ppermute(part, "rep", ZHI)
    total = part.astype(jnp.float32) + other.astype(jnp.float32)
    weights = jnp.stack([gate_weight, up_weight, down_weight]).reshape(rows, BLOCK)
    own_rows = lax.dynamic_slice_in_dim(weights, (core * NX + x) * share, share, 0)
    updated = (own_rows.astype(jnp.float32) + total / replicas).astype(jnp.bfloat16)
    half = lax.all_gather(updated, "rep", axis_index_groups=X_GROUPS, axis=0, tiled=True)
    other_half = lax.ppermute(half, "rep", CORE)
    both = jnp.where(
        core == 0,
        jnp.concatenate([half, other_half], axis=0),
        jnp.concatenate([other_half, half], axis=0),
    )
    result = both.reshape(3, *gate_weight.shape)
    return result[0], result[1], result[2]


def solution(mesh):
    return jax.shard_map(
        per_device,
        mesh=mesh,
        in_specs=(
            P("rep", "hid"),
            P("rep", "hid"),
            P("rep", None),
            P("hid", None),
            P("hid", None),
            P("hid"),
            P("hid", None, None, None),
            P("hid", None, None, None),
            P("hid", None, None, None),
        ),
        out_specs=(
            P("hid", None, None, None),
            P("hid", None, None, None),
            P("hid", None, None, None),
        ),
        check_vma=False,
    )
```

```python
import jax
import jax.numpy as jnp
import numpy as np
from jax import lax
from jax.experimental import pallas as pl
from jax.experimental.pallas import tpu as pltpu
from jax.sharding import PartitionSpec as P


D = 8192
FF = 16384
BLOCK = 128
LEVELS = 5
SEGS = 8
NZ, NY = 8, 4
NH, NX, NC = 2, 4, 2
VMEM = pl.BlockSpec(memory_space=pltpu.VMEM)
ANY = pl.BlockSpec(memory_space=pl.ANY)
SMEM = pl.BlockSpec(memory_space=pltpu.SMEM)
learn_rate = 8.0
max_rms = 0.1


def hid_pairs(move):
    pairs = []
    for z in range(NZ):
        for y in range(NY):
            to = move(z, y)
            if to is not None:
                pairs.append((z * NY + y, to[0] * NY + to[1]))
    return pairs


def rep_id(h, x, c):
    return (h * NX + x) * NC + c


def rep_pairs(move):
    return [
        (rep_id(h, x, c), rep_id(*move(h, x, c)))
        for h in range(NH)
        for x in range(NX)
        for c in range(NC)
    ]


HALF = NZ // 2
LOCAL = D // BLOCK // (NZ * NY)
PER_PLANE = 2 * LOCAL


def plane_order(z):
    first = min(max(z - 2, 0), HALF)
    order = list(range(first, first + HALF))
    return order + [p for p in range(NZ) if p not in order]


ORDER = [plane_order(z) for z in range(NZ)]
FAR = [[p - z for p in ORDER[z]] for z in range(NZ)]


def place_row(z):
    slots = [ORDER[z].index(p) for p in range(NZ)]
    return [((s // HALF) * NY * HALF + s % HALF) * PER_PLANE for s in slots] + FAR[z]


PLACES = np.array([place_row(z) for z in range(NZ)], np.int32)
Y_FAR = hid_pairs(lambda z, y: (z, (y + 2) % NY))


UP = hid_pairs(lambda z, y: (z + 1, y) if z < NZ - 1 else None)
DOWN = hid_pairs(lambda z, y: (z - 1, y) if z > 0 else None)
Y_NEXT = hid_pairs(lambda z, y: (z, (y + 1) % NY))
Y_PREV = hid_pairs(lambda z, y: (z, (y - 1) % NY))
CORE = rep_pairs(lambda h, x, c: (h, x, 1 - c))
ZHI = rep_pairs(lambda h, x, c: (1 - h, x, c))
Y_GROUPS = [[z * NY + y for y in range(NY)] for z in range(NZ)]
Z_GROUPS = [[z * NY + y for z in range(NZ)] for y in range(NY)]
X_GROUPS = [[rep_id(h, x, c) for x in range(NX)] for h in range(NH) for c in range(NC)]


def y_direct(own):
    left = lax.ppermute(own, "hid", Y_NEXT)
    right = lax.ppermute(own, "hid", Y_PREV)
    far = lax.ppermute(own, "hid", Y_FAR)
    return own, right, far, left


def y_ring(a, b):
    left_a = lax.ppermute(a, "hid", Y_NEXT)
    right_b = lax.ppermute(b, "hid", Y_PREV)
    left_b = lax.ppermute(b, "hid", Y_NEXT)
    right_a = lax.ppermute(a, "hid", Y_PREV)
    far_a = lax.ppermute(left_a, "hid", Y_NEXT)
    far_b = lax.ppermute(right_b, "hid", Y_PREV)
    return a, b, right_a, right_b, far_a, far_b, left_a, left_b


def prep_kernel(tokens_in, cotangent_in, seq_in, out, tokens, cotangent, seq, sems):
    pairs = ((seq_in, seq), (cotangent_in, cotangent), (tokens_in, tokens))
    copies = [pltpu.make_async_copy(a, b, sems.at[k]) for k, (a, b) in enumerate(pairs)]
    for copy in copies:
        copy.start()
    for copy in copies:
        copy.wait()
    count = tokens.shape[0]
    along = jnp.broadcast_to(seq[...].astype(jnp.float32), (count, count))
    same = (along == along.T).astype(jnp.float32)
    weight = count / (SEGS * jnp.sum(same, axis=1, keepdims=True))
    scaled = (cotangent[...].astype(jnp.float32) * weight).astype(jnp.bfloat16)
    for k in range(LOCAL):
        columns = slice(k * BLOCK, (k + 1) * BLOCK)
        out[k] = tokens[:, columns]
        out[LOCAL + k] = scaled[:, columns]


def pick(places, slots, chain, parts):
    wanted = [sorted({FAR[z][slot] for z in range(NZ)}) for slot in slots]
    far = sorted(set().union(*wanted))
    shape = chain[far[0]].shape
    each = len(slots) // parts

    def kernel(places, *refs):
        outs, sems = refs[len(far) : -1], refs[-1]
        for act in ("start", "wait"):
            for i, slot in enumerate(slots):
                mine = places[0, NZ + slot]
                for f in wanted[i]:

                    @pl.when(mine == f)
                    def _(i=i, f=f, act=act):
                        to = outs[i // each].at[pl.ds(i % each * PER_PLANE, PER_PLANE)]
                        copy = pltpu.make_async_copy(refs[far.index(f)], to, sems.at[i])
                        getattr(copy, act)()

    out = jax.ShapeDtypeStruct((each * PER_PLANE, *shape[1:]), jnp.bfloat16)
    return pl.pallas_call(
        kernel,
        out_shape=(out,) * parts,
        in_specs=[SMEM] + [ANY] * len(far),
        out_specs=(VMEM,) * parts,
        scratch_shapes=[pltpu.SemaphoreType.DMA((len(slots),))],
        compiler_params=pltpu.CompilerParams(vmem_limit_bytes=8 << 20),
        name="pick",
    )(places, *[chain[f] for f in far])


def ffn_kernel(in_scale, out_scale, n_bufs, places, here, in_blocks, out_blocks, *refs):
    bufs = refs[:n_bufs]
    wg, wu, wd, gain, mine, other, sq_out, big, sems = refs[n_bufs:]
    start, copies = 0, []
    for k, buf in enumerate(bufs):
        n = buf.shape[0]
        copies.append(pltpu.make_async_copy(buf, big.at[pl.ds(start, n)], sems.at[k]))
        start += n
    for copy in copies:
        copy.start()
    for copy in copies:
        copy.wait()

    def place(blocks, h, l, kind):
        block = blocks[h, l]
        owner = block // LOCAL
        plane = owner // NY
        side = (owner % NY - here[0] + NY) % NY
        return places[0, plane] + side * (HALF * PER_PLANE) + kind * LOCAL + block % LOCAL

    acc = jnp.zeros((1, 1), jnp.float32)
    count = wg.shape[0]
    for turn in range(count):
        h = (turn + here[1] * (count // 2)) % count
        grads = (mine, other)[turn // (count // 2)]
        at = turn % (count // 2)
        x = jnp.concatenate([big[place(in_blocks, h, l, 0)] for l in range(LEVELS)], axis=1)
        s = jnp.concatenate([big[place(out_blocks, h, l, 1)] for l in range(LEVELS)], axis=1)
        w_in = jnp.concatenate(
            [wg[h].reshape(LEVELS * BLOCK, BLOCK), wu[h].reshape(LEVELS * BLOCK, BLOCK)], axis=1
        )
        pre = jnp.dot(x, w_in, preferred_element_type=jnp.float32) * in_scale
        gate, up = pre[:, :BLOCK], pre[:, BLOCK:]
        g = gain[h]
        sig = jax.nn.sigmoid(gate)
        silu = gate * sig
        hidden = (silu * up * g).astype(jnp.bfloat16)
        w_out = jnp.concatenate([wd[h, l] for l in range(LEVELS)], axis=1)
        d_hidden = (
            lax.dot_general(s, w_out, (((1,), (1,)), ((), ())), preferred_element_type=jnp.float32)
            * out_scale
        )
        g_down = (
            lax.dot_general(hidden, s, (((0,), (0,)), ((), ())), preferred_element_type=jnp.float32)
            * out_scale
        )
        d_scaled = d_hidden * g
        d_gate = (d_scaled * up * sig * (1.0 + gate * (1.0 - sig))).astype(jnp.bfloat16)
        d_up = (d_scaled * silu).astype(jnp.bfloat16)
        d_both = jnp.concatenate([d_gate, d_up], axis=1)
        g_in = (
            lax.dot_general(x, d_both, (((0,), (0,)), ((), ())), preferred_element_type=jnp.float32)
            * in_scale
        )
        acc = acc + jnp.sum(jnp.sum(g_in * g_in, axis=0, keepdims=True), axis=1, keepdims=True)
        acc = acc + jnp.sum(jnp.sum(g_down * g_down, axis=0, keepdims=True), axis=1, keepdims=True)
        for l in range(LEVELS):
            rows = slice(l * BLOCK, (l + 1) * BLOCK)
            grads[0, at, l] = g_in[rows, :BLOCK].astype(jnp.bfloat16)
            grads[1, at, l] = g_in[rows, BLOCK:].astype(jnp.bfloat16)
            grads[2, at, l] = g_down[:, rows].astype(jnp.bfloat16)
    sq_out[...] = jnp.broadcast_to(acc, sq_out.shape)


def join_kernel(core, half, other, *refs):
    outs, sems = refs[:-1], refs[-1]
    n = half.shape[1]
    copies = []
    for k, out in enumerate(outs):
        copies.append(
            pltpu.make_async_copy(half.at[k], out.at[pl.ds(core[0] * n, n)], sems.at[2 * k])
        )
        copies.append(
            pltpu.make_async_copy(
                other.at[k], out.at[pl.ds((1 - core[0]) * n, n)], sems.at[2 * k + 1]
            )
        )
    for copy in copies:
        copy.start()
    for copy in copies:
        copy.wait()


def per_device(
    tokens,
    cotangent,
    seq_ids,
    in_blocks,
    out_blocks,
    unit_scale,
    gate_weight,
    up_weight,
    down_weight,
):
    tok_count = tokens.shape[0]
    blocks_dev = gate_weight.shape[0]
    hid, rep = lax.axis_index("hid"), lax.axis_index("rep")
    z, y = hid // NY, hid % NY
    core, x = rep % NC, (rep // NC) % NX

    places = lax.dynamic_slice_in_dim(jnp.asarray(PLACES), z, 1, 0)
    own = pl.pallas_call(
        prep_kernel,
        out_shape=jax.ShapeDtypeStruct((PER_PLANE, tok_count, BLOCK), jnp.bfloat16),
        in_specs=[ANY] * 3,
        out_specs=VMEM,
        scratch_shapes=[
            pltpu.VMEM(tokens.shape, tokens.dtype),
            pltpu.VMEM(cotangent.shape, cotangent.dtype),
            pltpu.VMEM(seq_ids.shape, seq_ids.dtype),
            pltpu.SemaphoreType.DMA((3,)),
        ],
        compiler_params=pltpu.CompilerParams(vmem_limit_bytes=8 << 20),
        name="prep",
    )(tokens, cotangent, seq_ids)
    chain = {0: own}
    for step in range(1, NZ):
        chain[-step] = lax.ppermute(chain[1 - step], "hid", UP)
        chain[step] = lax.ppermute(chain[step - 1], "hid", DOWN)
    bufs = y_direct(*pick(places, range(HALF), chain, 1))
    bufs += y_ring(*pick(places, range(HALF, NZ), chain, 2))

    in_scale = (LEVELS * BLOCK) ** (-0.5)
    out_scale = (LEVELS * BLOCK * (FF // D)) ** (-0.5)

    def kernel(*refs):
        ffn_kernel(in_scale, out_scale, len(bufs), *refs)

    half_shape = (3, blocks_dev // NC, *gate_weight.shape[1:])
    mine, other, local_sq = pl.pallas_call(
        kernel,
        out_shape=(
            jax.ShapeDtypeStruct(half_shape, jnp.bfloat16),
            jax.ShapeDtypeStruct(half_shape, jnp.bfloat16),
            jax.ShapeDtypeStruct((8, BLOCK), jnp.float32),
        ),
        in_specs=[SMEM] * 4 + [ANY] * len(bufs) + [VMEM] * 4,
        out_specs=(VMEM, VMEM, VMEM),
        scratch_shapes=[
            pltpu.VMEM((sum(b.shape[0] for b in bufs), tok_count, BLOCK), jnp.bfloat16),
            pltpu.SemaphoreType.DMA((len(bufs),)),
        ],
        compiler_params=pltpu.CompilerParams(vmem_limit_bytes=40 << 20),
        name="ffn",
    )(
        places,
        jnp.stack([y, core]),
        in_blocks,
        out_blocks,
        *bufs,
        gate_weight,
        up_weight,
        down_weight,
        unit_scale.reshape(blocks_dev, 1, BLOCK),
    )

    replicas = NH * NX * NC
    rows = 3 * blocks_dev // NC * LEVELS * BLOCK
    share = rows // NX
    partner = lax.ppermute(other.reshape(rows, BLOCK), "rep", CORE)
    half_tile = lax.broadcasted_iota(jnp.int32, local_sq.shape, 0) < local_sq.shape[0] // 2
    sums = jnp.where(half_tile, local_sq, lax.ppermute(local_sq, "rep", CORE))
    for groups in (Y_GROUPS, Z_GROUPS):
        n = len(groups[0])
        every = lax.all_to_all(
            jnp.broadcast_to(sums[None], (n, *sums.shape)),
            "hid", 0, 0, axis_index_groups=groups, tiled=True,
        )
        sums = every.sum(axis=0)
    own_sq, partner_sq = sums[:1], sums[-1:]
    count_all = 3 * (FF // BLOCK) * LEVELS * BLOCK * BLOCK

    def step_size(sq):
        rms_value = jnp.sqrt(sq[0, 0] / count_all + 1e-06)
        return -learn_rate * jnp.minimum(1.0, max_rms / rms_value)

    pair = (
        mine.reshape(rows, BLOCK).astype(jnp.float32) * step_size(own_sq)
        + partner.astype(jnp.float32) * step_size(partner_sq)
    ).astype(jnp.bfloat16)
    pieces = lax.all_to_all(
        pair.reshape(NX, share, BLOCK), "rep", 0, 0, axis_index_groups=X_GROUPS, tiled=True
    )
    part = pieces.astype(jnp.float32).sum(axis=0).astype(jnp.bfloat16)
    opposite = lax.ppermute(part, "rep", ZHI)
    total = part.astype(jnp.float32) + opposite.astype(jnp.float32)
    weights = jnp.stack(
        [
            lax.dynamic_slice_in_dim(w, core * (blocks_dev // NC), blocks_dev // NC, 0)
            for w in (gate_weight, up_weight, down_weight)
        ]
    ).reshape(rows, BLOCK)
    own_rows = lax.dynamic_slice_in_dim(weights, x * share, share, 0)
    updated = (own_rows.astype(jnp.float32) + total / replicas).astype(jnp.bfloat16)
    half = lax.all_gather(updated, "rep", axis_index_groups=X_GROUPS, axis=0, tiled=True)
    other_half = lax.ppermute(half, "rep", CORE)
    return pl.pallas_call(
        join_kernel,
        out_shape=(jax.ShapeDtypeStruct(gate_weight.shape, jnp.bfloat16),) * 3,
        in_specs=[SMEM, VMEM, VMEM],
        out_specs=(ANY,) * 3,
        scratch_shapes=[pltpu.SemaphoreType.DMA((6,))],
        compiler_params=pltpu.CompilerParams(vmem_limit_bytes=8 << 20),
        name="join",
    )(core.reshape(1), half.reshape(half_shape), other_half.reshape(half_shape))


def solution(mesh):
    return on_mesh(per_device, mesh)


def on_mesh(body, mesh):
    return jax.shard_map(
        body,
        mesh=mesh,
        in_specs=(
            P("rep", "hid"),
            P("rep", "hid"),
            P("rep", None),
            P("hid", None),
            P("hid", None),
            P("hid"),
            P("hid", None, None, None),
            P("hid", None, None, None),
            P("hid", None, None, None),
        ),
        out_specs=(
            P("hid", None, None, None),
            P("hid", None, None, None),
            P("hid", None, None, None),
        ),
        check_vma=False,
    )
```
